32 devices in a mesh: segment: 2 (over x), expert: 16 (over z, y, core).
Axes of the slice: x: 2, y: 2, z: 4, core: 2. Of those that a mesh axis runs over, the one named last changes fastest.
Arguments:
- fwd_prev: bfloat16 [2, 1024, 1536], P('segment', 'expert'), may hold values from -6 to 6
- bwd_prev: bfloat16 [2, 1024, 1536], P('segment', 'expert'), may hold values from -6 to 6
- stored_in: bfloat16 [2, 1024, 1536], P('segment', 'expert'), may hold values from -6 to 6
- fwd_routes: int32 [2, 1024, 4], P('segment', 'expert'), may hold values from 0 to 15, all different within a row; in each aligned block of 64 rows (0 to 63, 64 to 127, ..., all dimensions but the last counted through in order) at most 16 rows name the same one
- fwd_gates: float32 [2, 1024, 4], P('segment', 'expert'), may hold values from 0.05 to 1
- bwd_routes: int32 [2, 1024, 4], P('segment', 'expert'), may hold values from 0 to 15, all different within a row; in each aligned block of 64 rows (0 to 63, 64 to 127, ..., all dimensions but the last counted through in order) at most 16 rows name the same one
- bwd_gates: float32 [2, 1024, 4], P('segment', 'expert'), may hold values from 0.05 to 1
- norm_gain: float32 [2, 1536], P('segment'), may hold values from 0.1 to 1.9
- w_up: bfloat16 [2, 16, 1536, 1536], P('segment', 'expert'), may hold values from -0.15625 to 0.15625
- w_down: bfloat16 [2, 16, 1536, 1536], P('segment', 'expert'), may hold values from -0.15625 to 0.15625
Outputs:
- fwd_out: bfloat16 [2, 1024, 1536], P('segment', 'expert')
- bwd_out: bfloat16 [2, 1024, 1536], P('segment', 'expert')
The draws below stay inside these ranges and needn't reach their ends.
Inputs may be any that keep to these rules, and one draw needn't show every extreme that they name: `fwd_routes`: the 4 ids of a token differ. In each aligned block of 64 tokens of a segment (the tokens of one device), no expert is named by more than 16 tokens, a bound that some block reaches. `bwd_routes`: the 4 ids of a token differ. In each aligned block of 64 tokens of a segment (the tokens of one device), no expert is named by more than 16 tokens, a bound that some block reaches.
All inputs are finite; a program needn't handle non-finite values.
Results may differ from the reference program's by a relative error of at most 0.0048.
Values may be sent and summed in bfloat16 or wider, within the bound.
No kernel may reach another device: no remote copies, remote signals or barrier semaphores. Data moves between devices by JAX's collectives and lax.ppermute only.
A program may use at most 64 MiB of HBM per device.

```python
import math
import jax
import jax.numpy as jnp
import numpy as np
from jax import lax

D = 1536
FF = 1536
TOP = 4
TOK_DEV = 64
MOST = 16
EXPERTS = 16
TOKENS = 1024
N_SEGMENT = 2


def block_levels(rng, extent, pieces, low, high):
    level, own = 1.0, jax.random.fold_in(rng, 6)
    for dim, parts in pieces:
        draws = jnp.exp(jax.random.uniform(jax.random.fold_in(own, dim), (parts,), jnp.float32, low / len(pieces), high / len(pieces)))
        level = level * jnp.repeat(draws, extent[dim] // parts).reshape([-1 if axis == dim else 1 for axis in range(len(extent))])
    return level


def deal_out(own_key, own, number, rows, count, top, limit, slope):
    ranking = jax.random.permutation(own_key, count)
    packed, usual = shares(count, rows * top, limit, slope, True), shares(count, rows * top, limit, slope, False)
    places = jnp.arange(count)

    def named(lengths, rotation):
        used = int((lengths > 0).sum())
        fixed = max(1, used // 4)
        shifted = fixed + (places - fixed + rotation * (used - fixed)) % max(1, count - fixed)
        return jnp.zeros((count,), jnp.int32).at[ranking[jnp.where(places < fixed, places, shifted)]].set(jnp.asarray(lengths, jnp.int32))

    lengths = jnp.where(number % 4 == 0, named(packed, number // 4), named(usual, number - number // 4 - 1))
    mixed = jax.random.permutation(jax.random.fold_in(own, 3), count)
    donor, taker = mixed[0:count // 2 * 2:2], mixed[1:count // 2 * 2:2]
    margin = jnp.minimum(lengths[donor] - 1, limit - lengths[taker]) // 2
    margin = jnp.where((donor == ranking[0]) | (taker == ranking[0]) | (lengths[taker] == 0), 0, jnp.maximum(margin, 0))
    shifted = jax.random.randint(jax.random.fold_in(own, 4), (count // 2,), 0, 1 << 20) % (margin + 1)
    lengths = lengths.at[donor].add(-shifted).at[taker].add(shifted)
    items = jnp.searchsorted(jnp.cumsum(lengths), jnp.arange(rows * top), side="right").astype(jnp.int32)
    grid = items.reshape(top, rows).T
    grid = grid[jax.random.permutation(jax.random.fold_in(own, 1), rows)]
    rotation = jax.random.randint(jax.random.fold_in(own, 2), (rows, 1), 0, top)
    return jnp.take_along_axis(grid, (jnp.arange(top)[None, :] + rotation) % top, axis=1)


def shares(number_of, total, limit, slope, full):
    portions = [(1 << 20) // math.isqrt(standing ** slope) + 1 for standing in range(1, number_of + 1)]
    largest = limit if full else min(limit, max(-(-total // number_of), total * portions[0] // sum(portions)))
    least = 1 if total - largest >= number_of - 1 else 0
    holding, surplus = [largest] + [least] * (number_of - 1), total - largest - least * (number_of - 1)
    while surplus > 0:
        candidates = [i for i in range(1, number_of) if holding[i] < largest] or [i for i in range(1, number_of) if holding[i] < limit]
        mass, left = sum([portions[i] for i in candidates]), surplus
        for i in candidates:
            extra = min(limit - holding[i], max(1, left * portions[i] // mass), surplus)
            holding[i] = holding[i] + extra
            surplus = surplus - extra
    return np.array(holding)


def centred(own_key, dims, spread, reach, cuts=(), kind=jnp.bfloat16):
    result = jax.random.normal(own_key, dims, jnp.float32) * spread
    if len(cuts) > 0:
        result = block_levels(own_key, dims, cuts, -0.22, 0.18) * result
    return jnp.clip(result, min=-reach, max=reach).astype(kind)


def setup_inputs(seed: int = 0) -> dict:
    key_of = jax.random.split(jax.random.key(seed), 11)
    fwd_prev = centred(key_of[0], (N_SEGMENT, TOKENS, D), 1.0, 6.0, ((0, 2), (1, 16)))
    bwd_prev = centred(key_of[1], (N_SEGMENT, TOKENS, D), 1.0, 6.0, ((0, 2), (1, 16)))
    stored_in = centred(key_of[2], (N_SEGMENT, TOKENS, D), 1.0, 6.0, ((0, 2), (1, 16)))
    fwd_routes_keys = jax.random.split(jax.random.fold_in(key_of[3], 1), N_SEGMENT * TOKENS // TOK_DEV)
    fwd_routes_turns = jax.random.permutation(jax.random.fold_in(key_of[3], 3), N_SEGMENT * TOKENS // TOK_DEV)
    fwd_routes = jax.vmap(lambda own, number: deal_out(jax.random.fold_in(key_of[3], 2), own, number, TOK_DEV, EXPERTS, TOP, MOST, 2))(fwd_routes_keys, fwd_routes_turns).reshape((N_SEGMENT, TOKENS, TOP))
    fwd_gates = jnp.clip(jnp.exp(math.log(1.0) - 2.9957323 * jax.random.uniform(key_of[4], (N_SEGMENT, TOKENS, TOP), jnp.float32) ** block_levels(key_of[4], (N_SEGMENT, TOKENS, TOP), ((0, 2), (1, 16)), -0.2, 0.2)), 0.05, 1.0)
    bwd_routes_keys = jax.random.split(jax.random.fold_in(key_of[5], 1), N_SEGMENT * TOKENS // TOK_DEV)
    bwd_routes_turns = jax.random.permutation(jax.random.fold_in(key_of[5], 3), N_SEGMENT * TOKENS // TOK_DEV)
    bwd_routes = jax.vmap(lambda own, number: deal_out(jax.random.fold_in(key_of[5], 2), own, number, TOK_DEV, EXPERTS, TOP, MOST, 2))(bwd_routes_keys, bwd_routes_turns).reshape((N_SEGMENT, TOKENS, TOP))
    bwd_gates = jnp.clip(jnp.exp(math.log(1.0) - 2.9957323 * jax.random.uniform(key_of[6], (N_SEGMENT, TOKENS, TOP), jnp.float32) ** block_levels(key_of[6], (N_SEGMENT, TOKENS, TOP), ((0, 2), (1, 16)), -0.2, 0.2)), 0.05, 1.0)
    norm_gain = jnp.clip(1.0 + 0.18 * jax.random.normal(key_of[7], (N_SEGMENT, D), jnp.float32), 0.1, 1.9)
    w_up = centred(key_of[8], (N_SEGMENT, EXPERTS, D, FF), D ** -0.5, 0.15625, ((0, 2), (1, 16)))
    w_down = centred(key_of[9], (N_SEGMENT, EXPERTS, FF, D), FF ** -0.5, 0.15625, ((0, 2), (1, 16)))
    return {"fwd_prev": fwd_prev, "bwd_prev": bwd_prev, "stored_in": stored_in, "fwd_routes": fwd_routes, "fwd_gates": fwd_gates, "bwd_routes": bwd_routes, "bwd_gates": bwd_gates, "norm_gain": norm_gain, "w_up": w_up, "w_down": w_down}


norm_eps = 1e-05

def normalize(rows, gain):
    values = rows.astype(jnp.float32)
    scale = lax.rsqrt(lax.optimization_barrier(jnp.mean(values * values, axis=-1, keepdims=True)) + norm_eps)
    return (values, scale, (values * scale * gain).astype(jnp.bfloat16))

def expert_forward(rows, up_weight, down_weight):
    pre = jnp.dot(rows, up_weight, preferred_element_type=jnp.float32)
    act = jax.nn.silu(pre).astype(jnp.bfloat16)
    return jnp.dot(act, down_weight, preferred_element_type=jnp.float32).astype(jnp.bfloat16)

def expert_backward(rows, cotan, up_weight, down_weight):
    pre = jnp.dot(rows, up_weight, preferred_element_type=jnp.float32)
    sigma = jax.nn.sigmoid(pre)
    deriv = sigma * (1.0 + pre * (1.0 - sigma))
    back = lax.dot_general(cotan, down_weight, (((1,), (1,)), ((), ())), preferred_element_type=jnp.float32)
    inner = (back * deriv).astype(jnp.bfloat16)
    return lax.dot_general(inner, up_weight, (((1,), (1,)), ((), ())), preferred_element_type=jnp.float32).astype(jnp.bfloat16)

def placement_of(routes):
    flat = routes.reshape(-1).astype(jnp.int32)
    onehot = (flat[:, None] == jnp.arange(EXPERTS, dtype=jnp.int32)[None, :]).astype(jnp.int32)
    rank = lax.optimization_barrier(jnp.sum((jnp.cumsum(onehot, axis=0) - onehot) * onehot, axis=1))
    return (flat * (EXPERTS * MOST) + rank).astype(jnp.int32)

def dispatch(rows, dest):
    buffer = jnp.zeros((EXPERTS * EXPERTS * MOST, rows.shape[1]), rows.dtype)
    buffer = buffer.at[dest].set(jnp.repeat(rows, TOP, axis=0))
    return buffer.reshape(EXPERTS, EXPERTS * MOST, rows.shape[1])

def one_segment(items):
    arriving, cotangent, stored, f_routes, f_gates, b_routes, b_gates, gain, up_all, down_all = items
    f_values, f_scale, f_normed = normalize(arriving, gain)
    b_values, b_scale, b_normed = normalize(stored, gain)
    f_dest = placement_of(f_routes)
    b_dest = placement_of(b_routes)
    f_buf = dispatch(f_normed, f_dest)
    b_buf = dispatch(b_normed, b_dest)
    c_buf = dispatch(cotangent, b_dest)

    def serve(group):
        rows_f, rows_b, rows_c, up_weight, down_weight = group
        return (expert_forward(rows_f, up_weight, down_weight), expert_backward(rows_b, rows_c, up_weight, down_weight))
    f_res, b_res = lax.map(serve, (f_buf, b_buf, c_buf, up_all, down_all))
    f_rows = f_res.reshape(-1, D)[f_dest].reshape(TOKENS, TOP, D).astype(jnp.float32)
    b_rows = b_res.reshape(-1, D)[b_dest].reshape(TOKENS, TOP, D).astype(jnp.float32)
    fwd_out = (f_values + lax.optimization_barrier(jnp.sum(f_gates[:, :, None] * f_rows, axis=1))).astype(jnp.bfloat16)
    weighted = gain * lax.optimization_barrier(jnp.sum(b_gates[:, :, None] * b_rows, axis=1))
    correction = b_values * b_scale ** 3 * lax.optimization_barrier(jnp.mean(b_values * weighted, axis=-1, keepdims=True))
    bwd_out = (cotangent.astype(jnp.float32) + b_scale * weighted - correction).astype(jnp.bfloat16)
    return (fwd_out, bwd_out)

def reference(fwd_prev, bwd_prev, stored_in, fwd_routes, fwd_gates, bwd_routes, bwd_gates, norm_gain, w_up, w_down):
    arriving = jnp.roll(fwd_prev, 1, axis=0)
    cotangent = jnp.roll(bwd_prev, -1, axis=0)
    fwd_out, bwd_out = lax.map(one_segment, (arriving, cotangent, stored_in, fwd_routes, fwd_gates, bwd_routes, bwd_gates, norm_gain, w_up, w_down))
    return (fwd_out, bwd_out)
```

```python
import jax
import jax.numpy as jnp
from jax import lax
from jax.sharding import PartitionSpec as P

MOST = 16
norm_eps = 1e-05


def normalize(rows, gain):
    values = rows.astype(jnp.float32)
    scale = lax.rsqrt(jnp.mean(values * values, axis=-1, keepdims=True) + norm_eps)
    return (values, scale, (values * scale * gain).astype(jnp.bfloat16))


def expert_forward(rows, up_weight, down_weight):
    pre = jnp.dot(rows, up_weight, preferred_element_type=jnp.float32)
    act = jax.nn.silu(pre).astype(jnp.bfloat16)
    return jnp.dot(act, down_weight, preferred_element_type=jnp.float32).astype(jnp.bfloat16)


def expert_backward(rows, cotan, up_weight, down_weight):
    pre = jnp.dot(rows, up_weight, preferred_element_type=jnp.float32)
    sigma = jax.nn.sigmoid(pre)
    deriv = sigma * (1.0 + pre * (1.0 - sigma))
    back = lax.dot_general(
        cotan, down_weight, (((1,), (1,)), ((), ())), preferred_element_type=jnp.float32
    )
    inner = (back * deriv).astype(jnp.bfloat16)
    return lax.dot_general(
        inner, up_weight, (((1,), (1,)), ((), ())), preferred_element_type=jnp.float32
    ).astype(jnp.bfloat16)


class Layout:
    def __init__(self, experts, segments):
        self.experts = experts
        self.segments = segments
        self.half = experts // 2
        self.chips = experts // 4

    def hop(self, chip, step):
        if self.chips & (self.chips - 1) == 0:
            return chip ^ step
        return (chip + step) % self.chips

    def unhop(self, chip, step):
        if self.chips & (self.chips - 1) == 0:
            return chip ^ step
        return (chip - step) % self.chips

    def mid(self, value):
        pairs = [(e, (e + self.half) % self.experts) for e in range(self.experts)]
        return lax.ppermute(value, "expert", pairs)

    def core(self, value):
        return lax.ppermute(value, "expert", [(e, e ^ 1) for e in range(self.experts)])

    def chip(self, value, step, back=False):
        move = self.unhop if back else self.hop
        pairs = []
        for e in range(self.experts):
            h, inside = divmod(e, self.half)
            pairs.append((e, h * self.half + move(inside // 2, step) * 2 + inside % 2))
        return lax.ppermute(value, "expert", pairs)

    def relay(self, value, steps, across):
        pairs = []
        for s in range(self.segments):
            for e in range(self.experts):
                target = (e + self.half) % self.experts if across else e
                pairs.append(
                    (s * self.experts + e, ((s + steps) % self.segments) * self.experts + target)
                )
        return lax.ppermute(value, ("segment", "expert"), pairs)


def marks(routes, experts):
    named = jnp.any(
        routes[:, None, :, :] == jnp.arange(experts, dtype=jnp.int32)[None, :, None, None], axis=-1
    ).astype(jnp.float32)
    count = routes.shape[1]
    before = (jnp.arange(count)[:, None] < jnp.arange(count)[None, :]).astype(jnp.float32)
    rank = jnp.einsum("set,tu->seu", named, before, preferred_element_type=jnp.float32)
    return named, jnp.where(named > 0, rank, -1.0)


def body(
    fwd_prev,
    bwd_prev,
    stored_in,
    fwd_routes,
    fwd_gates,
    bwd_routes,
    bwd_gates,
    norm_gain,
    w_up,
    w_down,
):
    experts = lax.axis_size("expert")
    lay = Layout(experts, lax.axis_size("segment"))
    gain = norm_gain[0]
    up_weight = w_up[0, 0]
    down_weight = w_down[0, 0]
    tokens, width = stored_in.shape[1], stored_in.shape[2]
    top = fwd_routes.shape[2]
    chips = lay.chips

    mine = lax.axis_index("expert")
    my_half = mine // lay.half
    my_chip = (mine % lay.half) // 2
    my_core = mine % 2

    meta = jnp.concatenate(
        [fwd_routes[0].astype(jnp.float32), fwd_gates[0], bwd_routes[0].astype(jnp.float32), bwd_gates[0]],
        axis=1,
    )
    meta_mid = lay.mid(meta)
    meta_two = jnp.stack([meta, meta_mid])
    meta_four = jnp.concatenate([meta_two, lay.core(meta_two)])
    f_routes = meta_four[:, :, :top].astype(jnp.int32)
    f_gates = meta_two[:, :, top : 2 * top]
    b_routes = meta_four[:, :, 2 * top : 3 * top].astype(jnp.int32)
    b_gates = meta_two[:, :, 3 * top :]

    steps = jnp.arange(chips)
    chip_of = jnp.stack([lay.hop(my_chip, k) for k in range(chips)])
    near = my_half * lay.half + chip_of * 2 + my_core
    far = my_half * lay.half + chip_of * 2 + (1 - my_core)

    def plan(routes, gates):
        _, rank = marks(routes, experts)
        slot = jnp.arange(MOST, dtype=jnp.float32)
        near_rank = rank[:, near]
        far_rank = rank[:2, far]
        hit = near_rank[:, :, None, :] == slot[None, None, :, None]
        pack = jnp.einsum("skjt,su->ksjut", hit.astype(jnp.bfloat16), jnp.eye(4, dtype=jnp.bfloat16))
        pack = pack.reshape(chips * 4 * MOST, 4 * tokens)
        weight = jnp.sum(
            jnp.where(routes[:2, None] == jnp.arange(experts)[None, :, None, None], gates[:, None], 0.0),
            axis=-1,
        )
        parts = []
        for which, r in ((near, near_rank[:2]), (far, far_rank)):
            w = jnp.where(r[:, :, None, :] == slot[None, None, :, None], weight[:, which][:, :, None, :], 0.0)
            parts.append(w)
        full = jnp.concatenate(parts, axis=1).reshape(2, 2 * chips * MOST, tokens)
        one = lax.reduce_precision(full, 8, 7)
        two = lax.reduce_precision(full - one, 8, 7)
        three = lax.reduce_precision(full - one - two, 8, 7)
        split = jnp.stack([one, two, three], axis=1).astype(jnp.bfloat16)
        return pack, split

    f_pack, f_split = plan(f_routes, f_gates)
    b_pack, b_split = plan(b_routes, b_gates)

    def with_core(own, across):
        two = jnp.concatenate([own, across])
        return jnp.concatenate([two, lay.core(two)])

    def dispatch(rows, pack):
        packed = jnp.dot(pack, rows, preferred_element_type=jnp.float32).astype(jnp.bfloat16)
        packed = packed.reshape(chips, 4 * MOST, width)
        return jnp.concatenate([packed[0]] + [lay.chip(packed[k], k) for k in range(1, chips)])

    def returned(out, split):
        out = out.reshape(chips, 4 * MOST, width)
        back = jnp.stack([out[0]] + [lay.chip(out[k], k, back=True) for k in range(1, chips)])
        back = back.reshape(chips, 2, 2 * MOST, width)
        other = lay.core(back[:, 1])
        both = jnp.concatenate([back[:, 0], other]).reshape(2 * chips, 2, MOST, width)

        def partial(source):
            slots = both[:, source].reshape(2 * chips * MOST, width)
            sums = lax.dot_general(
                split[source], slots, (((1,), (0,)), ((), ())), preferred_element_type=jnp.float32
            )
            return sums[0] + sums[1] + sums[2]

        across = lay.mid(partial(1).astype(jnp.bfloat16))
        return partial(0) + across.astype(jnp.float32)

    stored = stored_in[0]
    b_rows = with_core(stored, lay.mid(stored))
    cotangent = lay.relay(bwd_prev[0], -1, False)
    c_rows = with_core(cotangent, lay.relay(bwd_prev[0], -1, True))
    arriving = lay.relay(fwd_prev[0], 1, False)
    f_rows = with_core(arriving, lay.relay(fwd_prev[0], 1, True))

    at_b = dispatch(normalize(b_rows, gain)[2], b_pack)
    at_c = dispatch(c_rows, b_pack)
    at_f = dispatch(normalize(f_rows, gain)[2], f_pack)
    out_b = expert_backward(at_b, at_c, up_weight, down_weight)
    out_f = expert_forward(at_f, up_weight, down_weight)
    b_sum = returned(out_b, b_split)
    f_sum = returned(out_f, f_split)

    fwd_out = (arriving.astype(jnp.float32) + f_sum).astype(jnp.bfloat16)
    b_values, b_scale, _ = normalize(stored, gain)
    weighted = gain * b_sum
    correction = b_values * b_scale**3 * jnp.mean(b_values * weighted, axis=-1, keepdims=True)
    bwd_out = (cotangent.astype(jnp.float32) + b_scale * weighted - correction).astype(jnp.bfloat16)
    return (fwd_out[None], bwd_out[None])


def solution(mesh):
    return jax.shard_map(
        body,
        mesh=mesh,
        in_specs=(
            P("segment", "expert", None),
            P("segment", "expert", None),
            P("segment", "expert", None),
            P("segment", "expert", None),
            P("segment", "expert", None),
            P("segment", "expert", None),
            P("segment", "expert", None),
            P("segment", None),
            P("segment", "expert", None, None),
            P("segment", "expert", None, None),
        ),
        out_specs=(P("segment", "expert", None), P("segment", "expert", None)),
        check_vma=False,
    )
```
